32 devices in a mesh: comp: 2 (over core), gx: 4 (over y, x), gy: 4 (over z).
Axes of the slice: x: 2, y: 2, z: 4, core: 2. Of those that a mesh axis runs over, the one named last changes fastest.
Arguments:
- state: float32 [2, 8, 96, 3072], P('comp', None, 'gx', 'gy'), may hold values from -6 to 6
- response: float32 [2, 8, 3072], P('comp'), may hold values from -0.95 to 0
- diffusion: float32 [2, 96, 3072], P('comp', 'gx', 'gy'), may hold values from 0.02 to 0.24
- land_mask: int32 [96, 3072], P('gx', 'gy'), may hold values 0 or 1
- couple_src: int32 [2, 4, 4, 16, 128], P('comp', 'gx', 'gy'), may hold values from 0 to 18431
- couple_dst: int32 [2, 4, 4, 16, 128], P('comp', 'gx', 'gy'), may hold values from 0 to 18431
- couple_weight: float32 [2, 4, 4, 16, 128], P('comp', 'gx', 'gy'), may hold values from 0.1 to 1
- couple_count: int32 [2, 4, 4, 16], P('comp', 'gx', 'gy'), may hold values from 0 to 128, as said below
Outputs:
- final_state: float32 [2, 8, 96, 3072], P('comp', None, 'gx', 'gy')
The draws below stay inside these ranges and needn't reach their ends.
Inputs may be any that keep to these rules, and one draw needn't show every extreme that they name: `couple_count`: at most 128 live slots per ordered device pair; every sending device has one pair with exactly 128.
All inputs are finite; a program needn't handle non-finite values. No bound on the sum of `land_mask` on one device may be relied on, other than what follows from the above.
Results may differ from the reference program's by a relative error of at most 0.0095.
Values may be sent and summed in bfloat16 or wider, within the bound.
A program may use at most 128 MiB of HBM per device.

```python
import math
import jax
import jax.numpy as jnp
from jax import lax

LEV = 8
FC = 4
STEPS = 1
RD = 24
COLS = 3072
CAP = 128
CD = 768
ROWS = 96
NPEER = 16
N_GX = 4
N_GY = 4


def draw_couple_count(key, part):
    key_a = jax.random.fold_in(key, 11)
    key_b = jax.random.fold_in(key, 12)
    key_c = jax.random.fold_in(key, 13)
    first = jax.random.randint(key_a, (2, N_GX, N_GY, NPEER), 0, CAP + 1)
    second = jax.random.randint(key_b, (2, N_GX, N_GY, NPEER), 0, CAP + 1)
    counts = jnp.maximum(first, second)
    chosen = jax.random.randint(key_c, (2, N_GX, N_GY, 1), 0, NPEER)
    peers = jnp.arange(NPEER, dtype=jnp.int32)[None, None, None, :]
    return jnp.where(peers == chosen, CAP, counts).astype(jnp.int32)


def place_ends(drawn, own_key, smallest, largest):
    longest = drawn.shape.index(max(drawn.shape))
    spots = []
    for shift in (0, 1):
        where = [jax.random.randint(jax.random.fold_in(own_key, axis), (), 0, length) for axis, length in enumerate(drawn.shape)]
        where[longest] = (where[longest] + shift) % drawn.shape[longest]
        spots.append(tuple(where))
    return drawn.at[spots[0]].set(smallest).at[spots[1]].set(largest)


def levels(own_key, dims, cuts, low, largest):
    gain, own = 1.0, jax.random.fold_in(own_key, 6)
    for axis_at, blocks in cuts:
        heights = jnp.exp(jax.random.uniform(jax.random.fold_in(own, axis_at), (blocks,), jnp.float32, low / len(cuts), largest / len(cuts)))
        gain = gain * jnp.repeat(heights, dims[axis_at] // blocks).reshape([-1 if axis == axis_at else 1 for axis in range(len(dims))])
    return gain


def centred(rng, extent, width, limit, split=(), held_as=jnp.bfloat16):
    level = levels(rng, extent, split, -0.22, 0.18) if split else 1.0
    drawn = jax.random.normal(rng, extent, jnp.float32) * width * level
    return jnp.minimum(jnp.maximum(drawn, -limit), limit).astype(held_as)


def setup_inputs(seed: int = 0) -> dict:
    keys = jax.random.split(jax.random.key(seed), 9)
    return {
        "state": centred(keys[0], (2, LEV, ROWS, COLS), 1.0, 6.0, ((0, 2), (2, 4), (3, 4)), jnp.float32),
        "response": jnp.clip(-0.95 + 0.95 * jax.random.uniform(keys[1], (2, LEV, COLS), jnp.float32) ** levels(keys[1], (2, LEV, COLS), ((0, 2),), -0.2, 0.2), -0.95, 0.0),
        "diffusion": jnp.clip(jnp.exp(math.log(0.24) - 2.4849066 * jax.random.uniform(keys[2], (2, ROWS, COLS), jnp.float32) ** levels(keys[2], (2, ROWS, COLS), ((0, 2), (1, 4), (2, 4)), -0.2, 0.2)), 0.02, 0.24),
        "land_mask": place_ends((jax.random.randint(keys[3], (ROWS, COLS), 0, 4) < 3).astype(jnp.int32), jax.random.fold_in(keys[3], 1), 0, 1),
        "couple_src": place_ends(jax.random.randint(keys[4], (2, N_GX, N_GY, NPEER, CAP), 0, RD * CD), jax.random.fold_in(keys[4], 1), 0, (RD * CD) - 1).astype(jnp.int32),
        "couple_dst": place_ends(jax.random.randint(keys[5], (2, N_GX, N_GY, NPEER, CAP), 0, RD * CD), jax.random.fold_in(keys[5], 1), 0, (RD * CD) - 1).astype(jnp.int32),
        "couple_weight": jnp.clip(0.1 + 0.9 * jax.random.uniform(keys[6], (2, N_GX, N_GY, NPEER, CAP), jnp.float32) ** levels(keys[6], (2, N_GX, N_GY, NPEER, CAP), ((0, 2), (1, 4), (2, 4)), -0.2, 0.2), 0.1, 1.0),
        "couple_count": draw_couple_count(jax.random.fold_in(keys[8], 71), 0),
    }


def make_table(cols):
    rows_idx = jnp.arange(cols, dtype=jnp.int32)[:, None]
    wave_idx = jnp.arange(cols // 2, dtype=jnp.int32)[None, :]
    phase = (rows_idx * wave_idx) % cols
    angle = phase.astype(jnp.float32) * (2.0 * math.pi / cols)
    return jnp.concatenate([jnp.cos(angle), jnp.sin(angle)], axis=1).astype(jnp.bfloat16)


def reference(state, response, diffusion, land_mask, couple_src, couple_dst, couple_weight, couple_count):
    cells = RD * CD
    table = make_table(COLS)
    slot_idx = jnp.arange(CAP, dtype=jnp.int32)
    live = slot_idx[None, None, None, None, :] < couple_count[..., None]
    weights = jnp.where(live, couple_weight, jnp.float32(0.0)).reshape(2, NPEER, NPEER, CAP)
    src_idx = couple_src.reshape(2, NPEER, NPEER * CAP)
    dst_idx = couple_dst.reshape(2, NPEER, NPEER * CAP)
    keep = jnp.stack([jnp.ones((ROWS, COLS), jnp.float32), land_mask.astype(jnp.float32)])
    lead = jnp.arange(2 * FC * NPEER, dtype=jnp.int32).reshape(2, FC, NPEER, 1)
    global_idx = (lead * cells + dst_idx[:, None, :, :]).reshape(-1)
    for step in range(STEPS):
        surface = state[:, :FC].reshape(2, FC, N_GX, RD, N_GY, CD)
        blocks = surface.transpose(0, 1, 2, 4, 3, 5).reshape(2, FC, NPEER, cells)
        values = jnp.take_along_axis(blocks, jnp.broadcast_to(src_idx[:, None], (2, FC, NPEER, NPEER * CAP)), axis=3)
        values = values.reshape(2, FC, NPEER, NPEER, CAP) * weights[:, None]
        arrived = values[::-1].transpose(0, 1, 3, 2, 4).reshape(-1)
        updated = blocks.reshape(-1).at[global_idx].add(arrived)
        updated = updated.reshape(2, FC, N_GX, N_GY, RD, CD).transpose(0, 1, 2, 4, 3, 5).reshape(2, FC, ROWS, COLS)
        state = jnp.concatenate([updated, state[:, FC:]], axis=1)
        grid_bf = state.astype(jnp.bfloat16).reshape(-1, COLS)
        spec = jnp.dot(grid_bf, table, preferred_element_type=jnp.float32).reshape(2, LEV, ROWS, COLS)
        filtered = (spec * response[:, :, None, :]).astype(jnp.bfloat16).reshape(-1, COLS)
        incr = lax.dot_general(filtered, table, (((1,), (1,)), ((), ())), preferred_element_type=jnp.float32)
        incr = (incr * (2.0 / COLS)).astype(jnp.bfloat16).reshape(2, LEV, ROWS, COLS)
        state = state + incr.astype(jnp.float32)
        padded = jnp.pad(state, ((0, 0), (0, 0), (1, 1), (0, 0)))
        state = state + diffusion[:, None] * (padded[:, :, 2:] + padded[:, :, :-2] - 2.0 * state)
        state = state * keep[:, None]
    return state
```

```python
import math

import jax
import jax.numpy as jnp
from jax import lax
from jax.sharding import PartitionSpec as P

FC = 4


def extended(block, sides, width):
    for axis, dim in sides:
        count = lax.axis_size(axis)
        forward = [(i, i + 1) for i in range(count - 1)]
        backward = [(target, source) for source, target in forward]
        low = lax.ppermute(
            lax.slice_in_dim(block, block.shape[dim] - width, None, axis=dim), axis, forward
        )
        high = lax.ppermute(lax.slice_in_dim(block, 0, width, axis=dim), axis, backward)
        block = jnp.concatenate([low, block, high], axis=dim)
    return block


def partner(value, axis, stride):
    mask = 2**stride
    pairs = [(source, source ^ mask) for source in range(lax.axis_size(axis))]
    return lax.ppermute(value, axis, pairs)


def make_table(cols):
    split = 64 if cols % 64 == 0 else 1
    wave_idx = jnp.arange(cols // 2, dtype=jnp.int32)[None, :]
    scale = 2.0 * math.pi / cols

    def trig(rows_idx):
        angle = (rows_idx * wave_idx % cols).astype(jnp.float32) * scale
        return jnp.cos(angle), jnp.sin(angle)

    cos_hi, sin_hi = trig(jnp.arange(cols // split, dtype=jnp.int32)[:, None] * split)
    cos_lo, sin_lo = trig(jnp.arange(split, dtype=jnp.int32)[:, None])
    cos_hi, sin_hi = cos_hi[:, None], sin_hi[:, None]
    cos_lo, sin_lo = cos_lo[None], sin_lo[None]
    cos_all = cos_hi * cos_lo - sin_hi * sin_lo
    sin_all = sin_hi * cos_lo + cos_hi * sin_lo
    table = jnp.concatenate([cos_all, sin_all], axis=2).astype(jnp.bfloat16)
    return table.reshape(cols, cols)


def back_transform(filtered, table_part):
    return lax.dot_general(
        filtered, table_part, (((1,), (1,)), ((), ())), preferred_element_type=jnp.float32
    )


def circle_increment(circles, resp_part, table, scale):
    count, rows_part, cols_all = circles.shape
    spec = jnp.dot(circles.reshape(-1, cols_all), table, preferred_element_type=jnp.float32)
    spec = spec.reshape(count, rows_part, cols_all)
    filtered = (spec * resp_part[:, None, :]).astype(jnp.bfloat16)
    incr = (back_transform(filtered.reshape(-1, cols_all), table) * scale).astype(jnp.bfloat16)
    return incr.reshape(count, rows_part, cols_all)


def diffuse(fields, rate):
    padded = extended(fields.astype(jnp.bfloat16), (("gx", 1),), 1).astype(fields.dtype)
    return fields + rate[None] * (padded[:, 2:] + padded[:, :-2] - 2.0 * fields)


def local(
    state, response, diffusion, land_mask, couple_src, couple_dst, couple_weight, couple_count
):
    levels, rows_dev, cols_dev = (state.shape[1], state.shape[2], state.shape[3])
    groups_x = lax.axis_size("gx")
    groups_y = lax.axis_size("gy")
    peers = groups_x * groups_y
    slots = couple_src.shape[4]
    cells = rows_dev * cols_dev
    cols_all = cols_dev * groups_y
    per_level = levels // groups_y
    section = lax.axis_index("comp")
    keep = jnp.where(section == 1, land_mask.astype(jnp.float32), jnp.float32(1.0))
    table = make_table(cols_all)
    scale = 2.0 / cols_all
    src_idx = couple_src.reshape(peers, slots)
    dst_idx = couple_dst.reshape(peers, slots)
    live = jnp.arange(slots, dtype=jnp.int32)[None, :] < couple_count.reshape(peers, 1)
    weights = jnp.where(live, couple_weight.reshape(peers, slots), jnp.float32(0.0))
    first_level = lax.axis_index("gy") * per_level
    resp_mine = lax.dynamic_slice_in_dim(response[0], first_level, per_level, 0)
    rate = diffusion[0]
    fields = state[0]
    surface = fields[:FC].reshape(FC, cells)
    outgoing = jnp.transpose(surface[:, src_idx] * weights[None], (1, 0, 2))
    crossed = partner(outgoing, "comp", 0)
    arrived = lax.all_to_all(crossed, ("gx", "gy"), split_axis=0, concat_axis=0, tiled=True)
    incoming = jnp.transpose(arrived, (1, 0, 2))
    surface = surface.at[:, dst_idx].add(incoming)
    surf = surface.reshape(FC, rows_dev, cols_dev)
    fields = jnp.concatenate([surf, fields[FC:]], axis=0)
    grid_bf = fields.astype(jnp.bfloat16)
    circles = lax.all_to_all(grid_bf, "gy", split_axis=0, concat_axis=2, tiled=True)
    incr = circle_increment(circles, resp_mine, table, scale)
    incr = lax.all_to_all(incr, "gy", split_axis=2, concat_axis=0, tiled=True)
    fields = fields + incr.astype(jnp.float32)
    fields = diffuse(fields, rate) * keep[None]
    return fields[None]


def solution(mesh):
    return jax.shard_map(
        local,
        mesh=mesh,
        in_specs=(
            P("comp", None, "gx", "gy"),
            P("comp", None, None),
            P("comp", "gx", "gy"),
            P("gx", "gy"),
            P("comp", "gx", "gy", None, None),
            P("comp", "gx", "gy", None, None),
            P("comp", "gx", "gy", None, None),
            P("comp", "gx", "gy", None),
        ),
        out_specs=P("comp", None, "gx", "gy"),
        check_vma=False,
    )
```

```python
import math

import jax
import jax.numpy as jnp
from jax import lax
from jax.sharding import PartitionSpec as P

FC = 4


def extended(block, sides, width):
    for axis, dim in sides:
        count = lax.axis_size(axis)
        forward = [(i, i + 1) for i in range(count - 1)]
        backward = [(target, source) for source, target in forward]
        low = lax.ppermute(
            lax.slice_in_dim(block, block.shape[dim] - width, None, axis=dim), axis, forward
        )
        high = lax.ppermute(lax.slice_in_dim(block, 0, width, axis=dim), axis, backward)
        block = jnp.concatenate([low, block, high], axis=dim)
    return block


def partner(value, axis, stride):
    mask = 2**stride
    pairs = [(source, source ^ mask) for source in range(lax.axis_size(axis))]
    return lax.ppermute(value, axis, pairs)


def make_table(cols):
    split = 64 if cols % 64 == 0 else 1
    wave_idx = jnp.arange(cols // 2, dtype=jnp.int32)[None, :]
    scale = 2.0 * math.pi / cols

    def trig(rows_idx):
        angle = (rows_idx * wave_idx % cols).astype(jnp.float32) * scale
        return jnp.cos(angle), jnp.sin(angle)

    cos_hi, sin_hi = trig(jnp.arange(cols // split, dtype=jnp.int32)[:, None] * split)
    cos_lo, sin_lo = trig(jnp.arange(split, dtype=jnp.int32)[:, None])
    cos_hi, sin_hi = cos_hi[:, None], sin_hi[:, None]
    cos_lo, sin_lo = cos_lo[None], sin_lo[None]
    cos_all = cos_hi * cos_lo - sin_hi * sin_lo
    sin_all = sin_hi * cos_lo + cos_hi * sin_lo
    table = jnp.concatenate([cos_all, sin_all], axis=2).astype(jnp.bfloat16)
    return table.reshape(cols, cols)


def back_transform(filtered, table_part):
    return lax.dot_general(
        filtered, table_part, (((1,), (1,)), ((), ())), preferred_element_type=jnp.float32
    )


def circle_increment(circles, resp_part, table, scale):
    count, rows_part, cols_all = circles.shape
    spec = jnp.dot(circles.reshape(-1, cols_all), table, preferred_element_type=jnp.float32)
    spec = spec.reshape(count, rows_part, cols_all)
    filtered = (spec * resp_part[:, None, :]).astype(jnp.bfloat16)
    incr = (back_transform(filtered.reshape(-1, cols_all), table) * scale).astype(jnp.bfloat16)
    return incr.reshape(count, rows_part, cols_all)


def diffuse(fields, rate):
    padded = extended(fields.astype(jnp.bfloat16), (("gx", 1),), 1).astype(fields.dtype)
    return fields + rate[None] * (padded[:, 2:] + padded[:, :-2] - 2.0 * fields)


def split3(values):
    high = values.astype(jnp.bfloat16)
    rest = values - high.astype(jnp.float32)
    mid = rest.astype(jnp.bfloat16)
    low = (rest - mid.astype(jnp.float32)).astype(jnp.bfloat16)
    return jnp.concatenate([high, mid, low], axis=0)


def exact_dot(values, onehot):
    rows = values.shape[0]
    out = jnp.dot(split3(values), onehot, preferred_element_type=jnp.float32)
    return out[:rows] + out[rows : 2 * rows] + out[2 * rows :]


def gather_cells(surface, index):
    fc, rows_dev, cols_dev = surface.shape
    row, col = index // cols_dev, index % cols_dev
    onehot = (jnp.arange(cols_dev, dtype=jnp.int32)[:, None] == col[None, :]).astype(jnp.bfloat16)
    picked = exact_dot(surface.reshape(fc * rows_dev, cols_dev), onehot)
    picked = picked.reshape(fc, rows_dev, -1)
    mask = jnp.arange(rows_dev, dtype=jnp.int32)[:, None] == row[None, :]
    return jnp.sum(jnp.where(mask[None], picked, 0.0), axis=1)


def scatter_cells(values, index, rows_dev, cols_dev):
    fc = values.shape[0]
    row, col = index // cols_dev, index % cols_dev
    mask = jnp.arange(rows_dev, dtype=jnp.int32)[:, None] == row[None, :]
    spread = jnp.where(mask[None], values[:, None, :], 0.0).reshape(fc * rows_dev, -1)
    onehot = (col[:, None] == jnp.arange(cols_dev, dtype=jnp.int32)[None, :]).astype(jnp.bfloat16)
    return exact_dot(spread, onehot).reshape(fc, rows_dev, cols_dev)


def local(
    state, response, diffusion, land_mask, couple_src, couple_dst, couple_weight, couple_count
):
    levels, rows_dev, cols_dev = (state.shape[1], state.shape[2], state.shape[3])
    groups_x = lax.axis_size("gx")
    groups_y = lax.axis_size("gy")
    peers = groups_x * groups_y
    slots = couple_src.shape[4]
    cells = rows_dev * cols_dev
    cols_all = cols_dev * groups_y
    per_level = levels // groups_y
    section = lax.axis_index("comp")
    keep = jnp.where(section == 1, land_mask.astype(jnp.float32), jnp.float32(1.0))
    table = make_table(cols_all)
    scale = 2.0 / cols_all
    src_idx = couple_src.reshape(peers, slots)
    dst_idx = couple_dst.reshape(peers, slots)
    live = jnp.arange(slots, dtype=jnp.int32)[None, :] < couple_count.reshape(peers, 1)
    weights = jnp.where(live, couple_weight.reshape(peers, slots), jnp.float32(0.0))
    first_level = lax.axis_index("gy") * per_level
    resp_mine = lax.dynamic_slice_in_dim(response[0], first_level, per_level, 0)
    rate = diffusion[0]
    fields = state[0]
    surface = fields[:FC]
    picked = gather_cells(surface, src_idx.reshape(-1)).reshape(FC, peers, slots)
    outgoing = jnp.transpose(picked * weights[None], (1, 0, 2))
    crossed = partner(outgoing, "comp", 0)
    arrived = lax.all_to_all(crossed, ("gx", "gy"), split_axis=0, concat_axis=0, tiled=True)
    incoming = jnp.transpose(arrived, (1, 0, 2)).reshape(FC, peers * slots)
    surf = surface + scatter_cells(incoming, dst_idx.reshape(-1), rows_dev, cols_dev)
    fields = jnp.concatenate([surf, fields[FC:]], axis=0)
    grid_bf = fields.astype(jnp.bfloat16)
    circles = lax.all_to_all(grid_bf, "gy", split_axis=0, concat_axis=2, tiled=True)
    incr = circle_increment(circles, resp_mine, table, scale)
    incr = lax.all_to_all(incr, "gy", split_axis=2, concat_axis=0, tiled=True)
    fields = fields + incr.astype(jnp.float32)
    fields = diffuse(fields, rate) * keep[None]
    return fields[None]


def solution(mesh):
    return jax.shard_map(
        local,
        mesh=mesh,
        in_specs=(
            P("comp", None, "gx", "gy"),
            P("comp", None, None),
            P("comp", "gx", "gy"),
            P("gx", "gy"),
            P("comp", "gx", "gy", None, None),
            P("comp", "gx", "gy", None, None),
            P("comp", "gx", "gy", None, None),
            P("comp", "gx", "gy", None),
        ),
        out_specs=P("comp", None, "gx", "gy"),
        check_vma=False,
    )
```

```python
import math

import jax
import jax.numpy as jnp
from jax import lax
from jax.sharding import PartitionSpec as P

FC = 4


def extended(block, sides, width):
    for axis, dim in sides:
        count = lax.axis_size(axis)
        forward = [(i, i + 1) for i in range(count - 1)]
        backward = [(target, source) for source, target in forward]
        low = lax.ppermute(
            lax.slice_in_dim(block, block.shape[dim] - width, None, axis=dim), axis, forward
        )
        high = lax.ppermute(lax.slice_in_dim(block, 0, width, axis=dim), axis, backward)
        block = jnp.concatenate([low, block, high], axis=dim)
    return block


def partner(value, axis, stride):
    mask = 2**stride
    pairs = [(source, source ^ mask) for source in range(lax.axis_size(axis))]
    return lax.ppermute(value, axis, pairs)


def make_table(cols, rows):
    split = 64 if rows % 64 == 0 else 1
    wave_idx = jnp.arange(cols // 2, dtype=jnp.int32)[None, :]
    scale = 2.0 * math.pi / cols

    def trig(rows_idx):
        angle = (rows_idx * wave_idx % cols).astype(jnp.float32) * scale
        return jnp.cos(angle), jnp.sin(angle)

    cos_hi, sin_hi = trig(jnp.arange(rows // split, dtype=jnp.int32)[:, None] * split)
    cos_lo, sin_lo = trig(jnp.arange(split, dtype=jnp.int32)[:, None])
    cos_hi, sin_hi = cos_hi[:, None], sin_hi[:, None]
    cos_lo, sin_lo = cos_lo[None], sin_lo[None]
    cos_all = cos_hi * cos_lo - sin_hi * sin_lo
    sin_all = sin_hi * cos_lo + cos_hi * sin_lo
    table = jnp.concatenate([cos_all, sin_all], axis=2).astype(jnp.bfloat16)
    return table.reshape(rows, cols)


def back_transform(filtered, table_part):
    return lax.dot_general(
        filtered, table_part, (((1,), (1,)), ((), ())), preferred_element_type=jnp.float32
    )


def circle_increment(circles, resp_part, table, scale):
    count, rows_part, cols_all = circles.shape
    half = cols_all // 2
    grid = circles.reshape(-1, cols_all)
    lines = grid.shape[0]
    sign = jnp.where(jnp.arange(cols_all, dtype=jnp.int32) % 2 == 0, 1.0, -1.0)
    both = jnp.dot(
        jnp.concatenate([grid[:, :half], grid[:, half:]], axis=0),
        table,
        preferred_element_type=jnp.float32,
    )
    spec = both[:lines] + sign[None, :] * both[lines:]
    spec = spec.reshape(count, rows_part, cols_all)
    filtered = (spec * resp_part[:, None, :]).astype(jnp.bfloat16).reshape(lines, cols_all)
    flipped = filtered * sign.astype(jnp.bfloat16)[None, :]
    back = back_transform(jnp.concatenate([filtered, flipped], axis=0), table)
    incr = jnp.concatenate([back[:lines], back[lines:]], axis=1)
    incr = (incr * scale).astype(jnp.bfloat16)
    return incr.reshape(count, rows_part, cols_all)


def diffuse(fields, rate):
    padded = extended(fields.astype(jnp.bfloat16), (("gx", 1),), 1).astype(fields.dtype)
    return fields + rate[None] * (padded[:, 2:] + padded[:, :-2] - 2.0 * fields)


def split3(values):
    high = values.astype(jnp.bfloat16)
    rest = values - high.astype(jnp.float32)
    mid = rest.astype(jnp.bfloat16)
    low = (rest - mid.astype(jnp.float32)).astype(jnp.bfloat16)
    return jnp.concatenate([high, mid, low], axis=0)


def exact_dot(values, onehot):
    rows = values.shape[0]
    out = jnp.dot(split3(values), onehot, preferred_element_type=jnp.float32)
    return out[:rows] + out[rows : 2 * rows] + out[2 * rows :]


def gather_cells(surface, index):
    fc, rows_dev, cols_dev = surface.shape
    row, col = index // cols_dev, index % cols_dev
    onehot = (jnp.arange(cols_dev, dtype=jnp.int32)[:, None] == col[None, :]).astype(jnp.bfloat16)
    picked = exact_dot(surface.reshape(fc * rows_dev, cols_dev), onehot)
    picked = picked.reshape(fc, rows_dev, -1)
    mask = jnp.arange(rows_dev, dtype=jnp.int32)[:, None] == row[None, :]
    return jnp.sum(jnp.where(mask[None], picked, 0.0), axis=1)


def scatter_cells(values, index, rows_dev, cols_dev):
    fc = values.shape[0]
    row, col = index // cols_dev, index % cols_dev
    mask = jnp.arange(rows_dev, dtype=jnp.int32)[:, None] == row[None, :]
    spread = jnp.where(mask[None], values[:, None, :], 0.0).reshape(fc * rows_dev, -1)
    onehot = (col[:, None] == jnp.arange(cols_dev, dtype=jnp.int32)[None, :]).astype(jnp.bfloat16)
    return exact_dot(spread, onehot).reshape(fc, rows_dev, cols_dev)


def local(
    state, response, diffusion, land_mask, couple_src, couple_dst, couple_weight, couple_count
):
    levels, rows_dev, cols_dev = (state.shape[1], state.shape[2], state.shape[3])
    groups_x = lax.axis_size("gx")
    groups_y = lax.axis_size("gy")
    peers = groups_x * groups_y
    slots = couple_src.shape[4]
    cells = rows_dev * cols_dev
    cols_all = cols_dev * groups_y
    per_level = levels // groups_y
    section = lax.axis_index("comp")
    keep = jnp.where(section == 1, land_mask.astype(jnp.float32), jnp.float32(1.0))
    table = make_table(cols_all, cols_all // 2)
    scale = 2.0 / cols_all
    src_idx = couple_src.reshape(peers, slots)
    dst_idx = couple_dst.reshape(peers, slots)
    live = jnp.arange(slots, dtype=jnp.int32)[None, :] < couple_count.reshape(peers, 1)
    weights = jnp.where(live, couple_weight.reshape(peers, slots), jnp.float32(0.0))
    first_level = lax.axis_index("gy") * per_level
    resp_mine = lax.dynamic_slice_in_dim(response[0], first_level, per_level, 0)
    rate = diffusion[0]
    fields = state[0]
    surface = fields[:FC]
    picked = gather_cells(surface, src_idx.reshape(-1)).reshape(FC, peers, slots)
    outgoing = jnp.transpose(picked * weights[None], (1, 0, 2))
    crossed = partner(outgoing, "comp", 0)
    arrived = lax.all_to_all(crossed, ("gx", "gy"), split_axis=0, concat_axis=0, tiled=True)
    incoming = jnp.transpose(arrived, (1, 0, 2)).reshape(FC, peers * slots)
    surf = surface + scatter_cells(incoming, dst_idx.reshape(-1), rows_dev, cols_dev)
    fields = jnp.concatenate([surf, fields[FC:]], axis=0)
    grid_bf = fields.astype(jnp.bfloat16)
    circles = lax.all_to_all(grid_bf, "gy", split_axis=0, concat_axis=2, tiled=True)
    incr = circle_increment(circles, resp_mine, table, scale)
    incr = lax.all_to_all(incr, "gy", split_axis=2, concat_axis=0, tiled=True)
    fields = fields + incr.astype(jnp.float32)
    fields = diffuse(fields, rate) * keep[None]
    return fields[None]


def solution(mesh):
    return jax.shard_map(
        local,
        mesh=mesh,
        in_specs=(
            P("comp", None, "gx", "gy"),
            P("comp", None, None),
            P("comp", "gx", "gy"),
            P("gx", "gy"),
            P("comp", "gx", "gy", None, None),
            P("comp", "gx", "gy", None, None),
            P("comp", "gx", "gy", None, None),
            P("comp", "gx", "gy", None),
        ),
        out_specs=P("comp", None, "gx", "gy"),
        check_vma=False,
    )
```

```python
import math

import jax
import jax.numpy as jnp
from jax import lax
from jax.sharding import PartitionSpec as P

FC = 4


def extended(block, sides, width):
    for axis, dim in sides:
        count = lax.axis_size(axis)
        forward = [(i, i + 1) for i in range(count - 1)]
        backward = [(target, source) for source, target in forward]
        low = lax.ppermute(
            lax.slice_in_dim(block, block.shape[dim] - width, None, axis=dim), axis, forward
        )
        high = lax.ppermute(lax.slice_in_dim(block, 0, width, axis=dim), axis, backward)
        block = jnp.concatenate([low, block, high], axis=dim)
    return block


def partner(value, axis, stride):
    mask = 2**stride
    pairs = [(source, source ^ mask) for source in range(lax.axis_size(axis))]
    return lax.ppermute(value, axis, pairs)


def make_table(cols, rows):
    split = 64 if rows % 64 == 0 else 1
    wave_idx = jnp.arange(cols // 2, dtype=jnp.int32)[None, :]
    scale = 2.0 * math.pi / cols

    def trig(rows_idx):
        angle = (rows_idx * wave_idx % cols).astype(jnp.float32) * scale
        return jnp.cos(angle), jnp.sin(angle)

    cos_hi, sin_hi = trig(jnp.arange(rows // split, dtype=jnp.int32)[:, None] * split)
    cos_lo, sin_lo = trig(jnp.arange(split, dtype=jnp.int32)[:, None])
    cos_hi, sin_hi = cos_hi[:, None], sin_hi[:, None]
    cos_lo, sin_lo = cos_lo[None], sin_lo[None]
    cos_all = cos_hi * cos_lo - sin_hi * sin_lo
    sin_all = sin_hi * cos_lo + cos_hi * sin_lo
    table = jnp.concatenate([cos_all, sin_all], axis=2).astype(jnp.bfloat16)
    return table.reshape(rows, cols)


def back_transform(filtered, table_part):
    return lax.dot_general(
        filtered, table_part, (((1,), (1,)), ((), ())), preferred_element_type=jnp.float32
    )


def circle_increment(circles, resp_part, table, scale):
    count, rows_part, cols_all = circles.shape
    half = cols_all // 2
    grid = circles.reshape(-1, cols_all)
    lines = grid.shape[0]
    sign = jnp.where(jnp.arange(cols_all, dtype=jnp.int32) % 2 == 0, 1.0, -1.0)
    both = jnp.dot(
        jnp.concatenate([grid[:, :half], grid[:, half:]], axis=0),
        table,
        preferred_element_type=jnp.float32,
    )
    spec = both[:lines] + sign[None, :] * both[lines:]
    spec = spec.reshape(count, rows_part, cols_all)
    filtered = (spec * resp_part[:, None, :]).astype(jnp.bfloat16).reshape(lines, cols_all)
    flipped = filtered * sign.astype(jnp.bfloat16)[None, :]
    back = back_transform(jnp.concatenate([filtered, flipped], axis=0), table)
    incr = jnp.concatenate([back[:lines], back[lines:]], axis=1)
    incr = (incr * scale).astype(jnp.bfloat16)
    return incr.reshape(count, rows_part, cols_all)


def diffuse(fields, rate):
    padded = extended(fields.astype(jnp.bfloat16), (("gx", 1),), 1).astype(fields.dtype)
    return fields + rate[None] * (padded[:, 2:] + padded[:, :-2] - 2.0 * fields)


def split3(values):
    high = values.astype(jnp.bfloat16)
    rest = values - high.astype(jnp.float32)
    mid = rest.astype(jnp.bfloat16)
    low = (rest - mid.astype(jnp.float32)).astype(jnp.bfloat16)
    return jnp.concatenate([high, mid, low], axis=0)


def exact_dot(values, onehot):
    rows = values.shape[0]
    out = jnp.dot(split3(values), onehot, preferred_element_type=jnp.float32)
    return out[:rows] + out[rows : 2 * rows] + out[2 * rows :]


def gather_cells(surface, index):
    fc, rows_dev, cols_dev = surface.shape
    row, col = index // cols_dev, index % cols_dev
    onehot = (jnp.arange(cols_dev, dtype=jnp.int32)[:, None] == col[None, :]).astype(jnp.bfloat16)
    picked = exact_dot(surface.reshape(fc * rows_dev, cols_dev), onehot)
    picked = picked.reshape(fc, rows_dev, -1)
    mask = jnp.arange(rows_dev, dtype=jnp.int32)[:, None] == row[None, :]
    return jnp.sum(jnp.where(mask[None], picked, 0.0), axis=1)


def scatter_cells(values, index, rows_dev, cols_dev):
    fc = values.shape[0]
    row, col = index // cols_dev, index % cols_dev
    mask = jnp.arange(rows_dev, dtype=jnp.int32)[:, None] == row[None, :]
    spread = jnp.where(mask[None], values[:, None, :], 0.0).reshape(fc * rows_dev, -1)
    onehot = (col[:, None] == jnp.arange(cols_dev, dtype=jnp.int32)[None, :]).astype(jnp.bfloat16)
    return exact_dot(spread, onehot).reshape(fc, rows_dev, cols_dev)


def local(
    state, response, diffusion, land_mask, couple_src, couple_dst, couple_weight, couple_count
):
    levels, rows_dev, cols_dev = (state.shape[1], state.shape[2], state.shape[3])
    groups_x = lax.axis_size("gx")
    groups_y = lax.axis_size("gy")
    peers = groups_x * groups_y
    slots = couple_src.shape[4]
    cells = rows_dev * cols_dev
    cols_all = cols_dev * groups_y
    per_level = levels // groups_y
    section = lax.axis_index("comp")
    keep = jnp.where(section == 1, land_mask.astype(jnp.float32), jnp.float32(1.0))
    table = make_table(cols_all, cols_all // 2)
    scale = 2.0 / cols_all
    src_idx = couple_src.reshape(peers, slots)
    dst_idx = couple_dst.reshape(peers, slots)
    live = jnp.arange(slots, dtype=jnp.int32)[None, :] < couple_count.reshape(peers, 1)
    weights = jnp.where(live, couple_weight.reshape(peers, slots), jnp.float32(0.0))
    first_level = lax.axis_index("gy") * per_level
    resp_mine = lax.dynamic_slice_in_dim(response[0], first_level, per_level, 0)
    rate = diffusion[0]
    fields = state[0]
    surface = fields[:FC]
    picked = gather_cells(surface, src_idx.reshape(-1)).reshape(FC, peers, slots)
    outgoing = jnp.transpose(picked * weights[None], (1, 0, 2))
    other = (1 - section) * peers
    spread = jnp.concatenate([outgoing, outgoing], axis=0)
    target = jnp.arange(2 * peers, dtype=jnp.int32)[:, None, None] // peers == 1 - section
    spread = jnp.where(target, spread, jnp.float32(0.0))
    mixed = lax.all_to_all(spread, ("comp", "gx", "gy"), split_axis=0, concat_axis=0, tiled=True)
    arrived = lax.dynamic_slice_in_dim(mixed, other, peers, 0)
    incoming = jnp.transpose(arrived, (1, 0, 2)).reshape(FC, peers * slots)
    surf = surface + scatter_cells(incoming, dst_idx.reshape(-1), rows_dev, cols_dev)
    fields = jnp.concatenate([surf, fields[FC:]], axis=0)
    grid_bf = fields.astype(jnp.bfloat16)
    circles = lax.all_to_all(grid_bf, "gy", split_axis=0, concat_axis=2, tiled=True)
    incr = circle_increment(circles, resp_mine, table, scale)
    incr = lax.all_to_all(incr, "gy", split_axis=2, concat_axis=0, tiled=True)
    fields = fields + incr.astype(jnp.float32)
    fields = diffuse(fields, rate) * keep[None]
    return fields[None]


def solution(mesh):
    return jax.shard_map(
        local,
        mesh=mesh,
        in_specs=(
            P("comp", None, "gx", "gy"),
            P("comp", None, None),
            P("comp", "gx", "gy"),
            P("gx", "gy"),
            P("comp", "gx", "gy", None, None),
            P("comp", "gx", "gy", None, None),
            P("comp", "gx", "gy", None, None),
            P("comp", "gx", "gy", None),
        ),
        out_specs=P("comp", None, "gx", "gy"),
        check_vma=False,
    )
```

```python
import math

import jax
import jax.numpy as jnp
from jax import lax
from jax.sharding import PartitionSpec as P

FC = 4


def extended(block, sides, width):
    for axis, dim in sides:
        count = lax.axis_size(axis)
        forward = [(i, i + 1) for i in range(count - 1)]
        backward = [(target, source) for source, target in forward]
        low = lax.ppermute(
            lax.slice_in_dim(block, block.shape[dim] - width, None, axis=dim), axis, forward
        )
        high = lax.ppermute(lax.slice_in_dim(block, 0, width, axis=dim), axis, backward)
        block = jnp.concatenate([low, block, high], axis=dim)
    return block


def partner(value, axis, stride):
    mask = 2**stride
    pairs = [(source, source ^ mask) for source in range(lax.axis_size(axis))]
    return lax.ppermute(value, axis, pairs)


def make_table(cols, rows):
    split = 64 if rows % 64 == 0 else 1
    wave_idx = jnp.arange(cols // 2, dtype=jnp.int32)[None, :]
    scale = 2.0 * math.pi / cols

    def trig(rows_idx):
        angle = (rows_idx * wave_idx % cols).astype(jnp.float32) * scale
        return jnp.cos(angle), jnp.sin(angle)

    cos_hi, sin_hi = trig(jnp.arange(rows // split, dtype=jnp.int32)[:, None] * split)
    cos_lo, sin_lo = trig(jnp.arange(split, dtype=jnp.int32)[:, None])
    cos_hi, sin_hi = cos_hi[:, None], sin_hi[:, None]
    cos_lo, sin_lo = cos_lo[None], sin_lo[None]
    cos_all = cos_hi * cos_lo - sin_hi * sin_lo
    sin_all = sin_hi * cos_lo + cos_hi * sin_lo
    table = jnp.concatenate([cos_all, sin_all], axis=2).astype(jnp.bfloat16)
    return table.reshape(rows, cols)


def back_transform(filtered, table_part):
    return lax.dot_general(
        filtered, table_part, (((1,), (1,)), ((), ())), preferred_element_type=jnp.float32
    )


def circle_increment(blocks, resp_part, table, scale):
    parts, count, rows_part, cols_dev = blocks.shape
    cols_all = parts * cols_dev
    lines = count * rows_part
    sign = jnp.where(jnp.arange(cols_all, dtype=jnp.int32) % 2 == 0, 1.0, -1.0)
    grid = blocks.reshape(2, parts // 2, lines, cols_dev)
    both = lax.dot_general(
        grid,
        table.reshape(parts // 2, cols_dev, cols_all),
        (((1, 3), (0, 1)), ((), ())),
        preferred_element_type=jnp.float32,
    )
    spec = both[0] + sign[None, :] * both[1]
    spec = spec.reshape(count, rows_part, cols_all)
    filtered = (spec * resp_part[:, None, :]).astype(jnp.bfloat16).reshape(lines, cols_all)
    flipped = filtered * sign.astype(jnp.bfloat16)[None, :]
    back = back_transform(jnp.concatenate([filtered, flipped], axis=0), table)
    incr = (back * scale).astype(jnp.bfloat16).reshape(2, lines, parts // 2, cols_dev)
    return jnp.transpose(incr, (0, 2, 1, 3)).reshape(parts, lines, cols_dev)


def diffuse(fields, rate):
    padded = extended(fields.astype(jnp.bfloat16), (("gx", 1),), 1).astype(fields.dtype)
    return fields + rate[None] * (padded[:, 2:] + padded[:, :-2] - 2.0 * fields)


def split3(values):
    high = values.astype(jnp.bfloat16)
    rest = values - high.astype(jnp.float32)
    mid = rest.astype(jnp.bfloat16)
    low = (rest - mid.astype(jnp.float32)).astype(jnp.bfloat16)
    return jnp.concatenate([high, mid, low], axis=0)


def exact_dot(values, onehot):
    rows = values.shape[0]
    out = jnp.dot(split3(values), onehot, preferred_element_type=jnp.float32)
    return out[:rows] + out[rows : 2 * rows] + out[2 * rows :]


def gather_cells(surface, index):
    fc, rows_dev, cols_dev = surface.shape
    row, col = index // cols_dev, index % cols_dev
    onehot = (jnp.arange(cols_dev, dtype=jnp.int32)[:, None] == col[None, :]).astype(jnp.bfloat16)
    picked = exact_dot(surface.reshape(fc * rows_dev, cols_dev), onehot)
    picked = picked.reshape(fc, rows_dev, -1)
    mask = jnp.arange(rows_dev, dtype=jnp.int32)[:, None] == row[None, :]
    return jnp.sum(jnp.where(mask[None], picked, 0.0), axis=1)


def scatter_cells(values, index, rows_dev, cols_dev):
    fc = values.shape[0]
    row, col = index // cols_dev, index % cols_dev
    mask = jnp.arange(rows_dev, dtype=jnp.int32)[:, None] == row[None, :]
    spread = jnp.where(mask[None], values[:, None, :], 0.0).reshape(fc * rows_dev, -1)
    onehot = (col[:, None] == jnp.arange(cols_dev, dtype=jnp.int32)[None, :]).astype(jnp.bfloat16)
    return exact_dot(spread, onehot).reshape(fc, rows_dev, cols_dev)


def local(
    state, response, diffusion, land_mask, couple_src, couple_dst, couple_weight, couple_count
):
    levels, rows_dev, cols_dev = (state.shape[1], state.shape[2], state.shape[3])
    groups_x = lax.axis_size("gx")
    groups_y = lax.axis_size("gy")
    peers = groups_x * groups_y
    slots = couple_src.shape[4]
    cells = rows_dev * cols_dev
    cols_all = cols_dev * groups_y
    per_level = levels // groups_y
    section = lax.axis_index("comp")
    keep = jnp.where(section == 1, land_mask.astype(jnp.float32), jnp.float32(1.0))
    table = make_table(cols_all, cols_all // 2)
    scale = 2.0 / cols_all
    src_idx = couple_src.reshape(peers, slots)
    dst_idx = couple_dst.reshape(peers, slots)
    live = jnp.arange(slots, dtype=jnp.int32)[None, :] < couple_count.reshape(peers, 1)
    weights = jnp.where(live, couple_weight.reshape(peers, slots), jnp.float32(0.0))
    first_level = lax.axis_index("gy") * per_level
    resp_mine = lax.dynamic_slice_in_dim(response[0], first_level, per_level, 0)
    rate = diffusion[0]
    fields = state[0]
    surface = fields[:FC]
    picked = gather_cells(surface, src_idx.reshape(-1)).reshape(FC, peers, slots)
    outgoing = jnp.transpose(picked * weights[None], (1, 0, 2))
    other = (1 - section) * peers
    spread = jnp.concatenate([outgoing, outgoing], axis=0)
    target = jnp.arange(2 * peers, dtype=jnp.int32)[:, None, None] // peers == 1 - section
    spread = jnp.where(target, spread, jnp.float32(0.0))
    mixed = lax.all_to_all(spread, ("comp", "gx", "gy"), split_axis=0, concat_axis=0, tiled=True)
    arrived = lax.dynamic_slice_in_dim(mixed, other, peers, 0)
    incoming = jnp.transpose(arrived, (1, 0, 2)).reshape(FC, peers * slots)
    surf = surface + scatter_cells(incoming, dst_idx.reshape(-1), rows_dev, cols_dev)
    fields = jnp.concatenate([surf, fields[FC:]], axis=0)
    grid_bf = fields.astype(jnp.bfloat16)
    grid_bf = grid_bf.reshape(groups_y, per_level, rows_dev, cols_dev)
    circles = lax.all_to_all(grid_bf, "gy", split_axis=0, concat_axis=0, tiled=True)
    incr = circle_increment(circles, resp_mine, table, scale)
    incr = lax.all_to_all(incr, "gy", split_axis=0, concat_axis=0, tiled=True)
    incr = incr.reshape(levels, rows_dev, cols_dev)
    fields = fields + incr.astype(jnp.float32)
    fields = diffuse(fields, rate) * keep[None]
    return fields[None]


def solution(mesh):
    return jax.shard_map(
        local,
        mesh=mesh,
        in_specs=(
            P("comp", None, "gx", "gy"),
            P("comp", None, None),
            P("comp", "gx", "gy"),
            P("gx", "gy"),
            P("comp", "gx", "gy", None, None),
            P("comp", "gx", "gy", None, None),
            P("comp", "gx", "gy", None, None),
            P("comp", "gx", "gy", None),
        ),
        out_specs=P("comp", None, "gx", "gy"),
        check_vma=False,
    )
```

```python
import math

import jax
import jax.numpy as jnp
from jax import lax
from jax.sharding import PartitionSpec as P

FC = 4


def extended(block, sides, width):
    for axis, dim in sides:
        count = lax.axis_size(axis)
        forward = [(i, i + 1) for i in range(count - 1)]
        backward = [(target, source) for source, target in forward]
        low = lax.ppermute(
            lax.slice_in_dim(block, block.shape[dim] - width, None, axis=dim), axis, forward
        )
        high = lax.ppermute(lax.slice_in_dim(block, 0, width, axis=dim), axis, backward)
        block = jnp.concatenate([low, block, high], axis=dim)
    return block


def partner(value, axis, stride):
    mask = 2**stride
    pairs = [(source, source ^ mask) for source in range(lax.axis_size(axis))]
    return lax.ppermute(value, axis, pairs)


def make_table(cols, rows):
    split = 64 if rows % 64 == 0 else 1
    wave_idx = jnp.arange(cols // 2, dtype=jnp.int32)[None, :]
    scale = 2.0 * math.pi / cols

    def trig(rows_idx):
        angle = (rows_idx * wave_idx % cols).astype(jnp.float32) * scale
        return jnp.cos(angle), jnp.sin(angle)

    cos_hi, sin_hi = trig(jnp.arange(rows // split, dtype=jnp.int32)[:, None] * split)
    cos_lo, sin_lo = trig(jnp.arange(split, dtype=jnp.int32)[:, None])
    cos_hi, sin_hi = cos_hi[:, None], sin_hi[:, None]
    cos_lo, sin_lo = cos_lo[None], sin_lo[None]
    cos_all = cos_hi * cos_lo - sin_hi * sin_lo
    sin_all = sin_hi * cos_lo + cos_hi * sin_lo
    table = jnp.concatenate([cos_all, sin_all], axis=2).astype(jnp.bfloat16)
    return table.reshape(rows, cols)


def back_transform(filtered, table_part):
    return lax.dot_general(
        filtered, table_part, (((1,), (1,)), ((), ())), preferred_element_type=jnp.float32
    )


def circle_increment(blocks, resp_part, table, scale):
    parts, count, rows_part, cols_dev = blocks.shape
    cols_all = parts * cols_dev
    lines = count * rows_part
    sign = jnp.where(jnp.arange(cols_all, dtype=jnp.int32) % 2 == 0, 1.0, -1.0)
    grid = blocks.reshape(2, parts // 2, lines, cols_dev)
    both = lax.dot_general(
        grid,
        table.reshape(parts // 2, cols_dev, cols_all),
        (((1, 3), (0, 1)), ((), ())),
        preferred_element_type=jnp.float32,
    )
    spec = both[0] + sign[None, :] * both[1]
    spec = spec.reshape(count, rows_part, cols_all)
    filtered = (spec * resp_part[:, None, :]).astype(jnp.bfloat16).reshape(lines, cols_all)
    flipped = filtered * sign.astype(jnp.bfloat16)[None, :]
    back = back_transform(jnp.concatenate([filtered, flipped], axis=0), table)
    incr = (back * scale).astype(jnp.bfloat16).reshape(2, lines, parts // 2, cols_dev)
    return jnp.transpose(incr, (0, 2, 1, 3)).reshape(parts, lines, cols_dev)


def diffuse(fields, rate):
    count = lax.axis_size("gx")
    forward = [(i, i + 1) for i in range(count - 1)]
    backward = [(target, source) for source, target in forward]
    edge_low = lax.ppermute(fields[:, -1:].astype(jnp.bfloat16), "gx", forward)
    edge_high = lax.ppermute(fields[:, :1].astype(jnp.bfloat16), "gx", backward)
    above = jnp.concatenate([edge_low.astype(fields.dtype), fields[:, :-1]], axis=1)
    below = jnp.concatenate([fields[:, 1:], edge_high.astype(fields.dtype)], axis=1)
    return fields + rate[None] * (below + above - 2.0 * fields)


def split3(values):
    high = values.astype(jnp.bfloat16)
    rest = values - high.astype(jnp.float32)
    mid = rest.astype(jnp.bfloat16)
    low = (rest - mid.astype(jnp.float32)).astype(jnp.bfloat16)
    return jnp.concatenate([high, mid, low], axis=0)


def exact_dot(values, onehot):
    rows = values.shape[0]
    out = jnp.dot(split3(values), onehot, preferred_element_type=jnp.float32)
    return out[:rows] + out[rows : 2 * rows] + out[2 * rows :]


def gather_cells(surface, index):
    fc, rows_dev, cols_dev = surface.shape
    row, col = index // cols_dev, index % cols_dev
    onehot = (jnp.arange(cols_dev, dtype=jnp.int32)[:, None] == col[None, :]).astype(jnp.bfloat16)
    picked = exact_dot(surface.reshape(fc * rows_dev, cols_dev), onehot)
    picked = picked.reshape(fc, rows_dev, -1)
    mask = jnp.arange(rows_dev, dtype=jnp.int32)[:, None] == row[None, :]
    return jnp.sum(jnp.where(mask[None], picked, 0.0), axis=1)


def scatter_cells(values, index, rows_dev, cols_dev):
    fc = values.shape[0]
    row, col = index // cols_dev, index % cols_dev
    mask = jnp.arange(rows_dev, dtype=jnp.int32)[:, None] == row[None, :]
    spread = jnp.where(mask[None], values[:, None, :], 0.0).reshape(fc * rows_dev, -1)
    onehot = (col[:, None] == jnp.arange(cols_dev, dtype=jnp.int32)[None, :]).astype(jnp.bfloat16)
    return exact_dot(spread, onehot).reshape(fc, rows_dev, cols_dev)


def local(
    state, response, diffusion, land_mask, couple_src, couple_dst, couple_weight, couple_count
):
    levels, rows_dev, cols_dev = (state.shape[1], state.shape[2], state.shape[3])
    groups_x = lax.axis_size("gx")
    groups_y = lax.axis_size("gy")
    peers = groups_x * groups_y
    slots = couple_src.shape[4]
    cells = rows_dev * cols_dev
    cols_all = cols_dev * groups_y
    per_level = levels // groups_y
    section = lax.axis_index("comp")
    keep = jnp.where(section == 1, land_mask.astype(jnp.float32), jnp.float32(1.0))
    table = make_table(cols_all, cols_all // 2)
    scale = 2.0 / cols_all
    src_idx = couple_src.reshape(peers, slots)
    dst_idx = couple_dst.reshape(peers, slots)
    live = jnp.arange(slots, dtype=jnp.int32)[None, :] < couple_count.reshape(peers, 1)
    weights = jnp.where(live, couple_weight.reshape(peers, slots), jnp.float32(0.0))
    first_level = lax.axis_index("gy") * per_level
    resp_mine = lax.dynamic_slice_in_dim(response[0], first_level, per_level, 0)
    rate = diffusion[0]
    fields = state[0]
    surface = fields[:FC]
    picked = gather_cells(surface, src_idx.reshape(-1)).reshape(FC, peers, slots)
    outgoing = jnp.transpose(picked * weights[None], (1, 0, 2))
    other = (1 - section) * peers
    spread = jnp.concatenate([outgoing, outgoing], axis=0)
    target = jnp.arange(2 * peers, dtype=jnp.int32)[:, None, None] // peers == 1 - section
    spread = jnp.where(target, spread, jnp.float32(0.0))
    mixed = lax.all_to_all(spread, ("comp", "gx", "gy"), split_axis=0, concat_axis=0, tiled=True)
    arrived = lax.dynamic_slice_in_dim(mixed, other, peers, 0)
    incoming = jnp.transpose(arrived, (1, 0, 2)).reshape(FC, peers * slots)
    surf = surface + scatter_cells(incoming, dst_idx.reshape(-1), rows_dev, cols_dev)
    fields = jnp.concatenate([surf, fields[FC:]], axis=0)
    grid_bf = fields.astype(jnp.bfloat16)
    grid_bf = grid_bf.reshape(groups_y, per_level, rows_dev, cols_dev)
    circles = lax.all_to_all(grid_bf, "gy", split_axis=0, concat_axis=0, tiled=True)
    incr = circle_increment(circles, resp_mine, table, scale)
    incr = lax.all_to_all(incr, "gy", split_axis=0, concat_axis=0, tiled=True)
    incr = incr.reshape(levels, rows_dev, cols_dev)
    fields = fields + incr.astype(jnp.float32)
    fields = diffuse(fields, rate) * keep[None]
    return fields[None]


def solution(mesh):
    return jax.shard_map(
        local,
        mesh=mesh,
        in_specs=(
            P("comp", None, "gx", "gy"),
            P("comp", None, None),
            P("comp", "gx", "gy"),
            P("gx", "gy"),
            P("comp", "gx", "gy", None, None),
            P("comp", "gx", "gy", None, None),
            P("comp", "gx", "gy", None, None),
            P("comp", "gx", "gy", None),
        ),
        out_specs=P("comp", None, "gx", "gy"),
        check_vma=False,
    )
```
